32 devices in a mesh: row: 4 (over y, x), col: 8 (over z, core).
Axes of the slice: x: 2, y: 2, z: 4, core: 2. Of those that a mesh axis runs over, the one named last changes fastest.
Arguments:
- pair_rep: float32 [64, 64, 128], P('row', 'col'), may hold values from -160 to 160
- ln_gain: float32 [128], replicated, may hold values from 0.25 to 1.75
- ln_bias: float32 [128], replicated, may hold values from -3 to 3
- w_in: float32 [1024, 128], replicated, may hold values from -0.5 to 0.5
- w_out: float32 [512, 128], replicated, may hold values from -0.25 to 0.25
- w_pde: float32 [128, 64], replicated, may hold values from -2 to 2
- labels: int32 [64, 64], P('row', 'col'), may hold values from 0 to 63
- pair_mask: int32 [64, 64], P('row', 'col'), may hold values from 0 to 1, as said below
Outputs:
- mean_loss: float32 [], replicated
- d_pair_rep: float32 [64, 64, 128], P('row', 'col')
- d_ln_gain: float32 [128], replicated
- d_ln_bias: float32 [128], replicated
- d_w_in: float32 [1024, 128], P(('row', 'col'))
- d_w_out: float32 [512, 128], P(('row', 'col'))
- d_w_pde: float32 [128, 64], replicated
The draws below stay inside these ranges and needn't reach their ends.
Inputs may be any that keep to these rules, and one draw needn't show every extreme that they name: pair_mask[i][j] = m_i m_j for a flag m_i of token i, with m_i = 1 whenever i is a multiple of 16.
All inputs are finite; a program needn't handle non-finite values.
Results may differ from the reference program's by a relative error of at most 0.0003.
Values sent between devices are 32-bit elements; how exact they have to be, the bound alone decides.
A program may use at most 64 MiB of HBM per device.

```python
import jax
import jax.numpy as jnp
from jax import lax

C = 128
H = 512
BINS = 64
TOKENS = 64


def draw_pair_rep(key, part):
    keys = jax.random.split(jax.random.fold_in(key, 11), 1)
    values = jax.random.normal(keys[0], (TOKENS, TOKENS, C), jnp.float32)
    return jnp.clip(values, -6.0, 6.0)


def draw_w_pde(key, part):
    keys = jax.random.split(jax.random.fold_in(key, 23), 1)
    values = jax.random.normal(keys[0], (C, BINS), jnp.float32) * (2.5 / C ** 0.5)
    return jnp.clip(values, -2.0, 2.0)


def draw_pair_mask(key, part):
    position = jnp.arange(TOKENS, dtype=jnp.int32)
    threshold = 300 + 650 * position // TOKENS
    ticket = jax.random.randint(jax.random.fold_in(key, 37), (TOKENS,), 0, 1000, dtype=jnp.int32)
    resolved = jnp.logical_or(ticket < threshold, position % 16 == 0).astype(jnp.int32)
    return resolved[:, None] * resolved[None, :]


def with_ends(values, rng, smallest, high):
    place = [jax.random.randint(jax.random.fold_in(rng, axis), (), 0, length) for axis, length in enumerate(values.shape)]
    widest = values.shape.index(max(values.shape))
    beside = place[:widest] + [(place[widest] + 1) % values.shape[widest]] + place[widest + 1:]
    return values.at[tuple(place)].set(smallest).at[tuple(beside)].set(high)


def noise(rng, shape, deviation, limit, kind=jnp.bfloat16):
    array = deviation * jax.random.normal(rng, shape, jnp.float32)
    return jnp.clip(array, min=-limit, max=limit).astype(kind)


def setup_inputs(seed: int = 0) -> dict:
    seeds = jax.random.split(jax.random.key(seed), 9)
    pair_rep = draw_pair_rep(jax.random.fold_in(seeds[8], 71), 0)
    ln_gain = jnp.clip(1.0 + 0.15 * jax.random.normal(seeds[1], (C,), jnp.float32), 0.25, 1.75)
    ln_bias = noise(seeds[2], (C,), 0.5, 3.0, jnp.float32)
    w_in = noise(seeds[3], (2 * H, C), C ** -0.5, 0.5, jnp.float32)
    w_out = noise(seeds[4], (H, C), H ** -0.5, 0.25, jnp.float32)
    w_pde = draw_w_pde(jax.random.fold_in(seeds[8], 71), 0)
    labels = with_ends(jax.random.randint(seeds[6], (TOKENS, TOKENS), 0, BINS), jax.random.fold_in(seeds[6], 1), 0, BINS - 1).astype(jnp.int32)
    pair_mask = draw_pair_mask(jax.random.fold_in(seeds[8], 71), 0)
    return dict(pair_rep=pair_rep, ln_gain=ln_gain, ln_bias=ln_bias, w_in=w_in, w_out=w_out, w_pde=w_pde, labels=labels, pair_mask=pair_mask)


epsilon = 1e-05

def transition(rows_block, ln_gain, ln_bias, w_in, w_out):
    average = lax.optimization_barrier(jnp.mean(rows_block, axis=-1, keepdims=True))
    centred = rows_block - average
    variance = lax.optimization_barrier(jnp.mean(centred * centred, axis=-1, keepdims=True))
    normed = centred * lax.rsqrt(variance + epsilon) * ln_gain + ln_bias
    projected_in = lax.dot_general(normed, w_in, (((1,), (1,)), ((), ())), precision=lax.Precision.HIGHEST, preferred_element_type=jnp.float32)
    hidden_units = w_out.shape[0]
    hidden = jax.nn.silu(projected_in[:, :hidden_units]) * projected_in[:, hidden_units:]
    return rows_block + jnp.dot(hidden, w_out, precision=lax.Precision.HIGHEST, preferred_element_type=jnp.float32)

def group_rows(tile_rows, tile_cols):
    stride_rows = 1
    while stride_rows < tile_rows and stride_rows * tile_cols < 1024 and (tile_rows % (stride_rows * 2) == 0):
        stride_rows = stride_rows * 2
    return stride_rows

def reference(pair_rep, ln_gain, ln_bias, w_in, w_out, w_pde, labels, pair_mask):
    tokens_first, tokens_second, channels = pair_rep.shape
    stride_rows = group_rows(tokens_first, tokens_second)
    blocks = pair_rep.reshape(tokens_first // stride_rows, stride_rows * tokens_second, channels)

    def forward(rows_block):
        return transition(rows_block, ln_gain, ln_bias, w_in, w_out)
    updated = lax.map(forward, blocks).reshape(tokens_first, tokens_second, channels)
    projected = jnp.einsum('ijc,cb->ijb', updated, w_pde, precision=lax.Precision.HIGHEST)
    scores = projected + jnp.transpose(projected, (1, 0, 2))
    mask_float = pair_mask.astype(jnp.float32)
    valid_count = jnp.sum(mask_float)
    highest = lax.optimization_barrier(jnp.max(scores, axis=-1, keepdims=True))
    shifted = jnp.exp(scores - highest)
    exp_total = lax.optimization_barrier(jnp.sum(shifted, axis=-1, keepdims=True))
    log_total = highest + jnp.log(exp_total)
    picked = jnp.take_along_axis(scores, labels[:, :, None].astype(jnp.int32), axis=-1)
    mean_loss = jnp.sum(mask_float * (log_total - picked)[:, :, 0]) / valid_count
    bin_index = jnp.arange(scores.shape[2], dtype=jnp.int32)
    onehot = (labels[:, :, None] == bin_index[None, None, :]).astype(jnp.float32)
    d_scores = mask_float[:, :, None] * (shifted / exp_total - onehot) / valid_count
    d_sym = d_scores + jnp.transpose(d_scores, (1, 0, 2))
    d_w_pde = jnp.einsum('ijc,ijb->cb', updated, d_sym, precision=lax.Precision.HIGHEST)
    d_updated = jnp.einsum('ijb,cb->ijc', d_sym, w_pde, precision=lax.Precision.HIGHEST)
    cot_blocks = d_updated.reshape(blocks.shape)

    def backward(totals, pieces):
        rows_block, cotangent = pieces
        outcome, pullback = jax.vjp(transition, rows_block, ln_gain, ln_bias, w_in, w_out)
        gradients = pullback(cotangent)
        merged = tuple((earlier + later for earlier, later in zip(totals, gradients[1:])))
        return (merged, gradients[0])
    start_sums = (jnp.zeros_like(ln_gain), jnp.zeros_like(ln_bias), jnp.zeros_like(w_in), jnp.zeros_like(w_out))
    param_sums, d_blocks = lax.scan(backward, start_sums, (blocks, cot_blocks))
    d_pair_rep = d_blocks.reshape(pair_rep.shape)
    d_ln_gain = param_sums[0]
    d_ln_bias = param_sums[1]
    d_w_in = param_sums[2]
    d_w_out = param_sums[3]
    return (mean_loss, d_pair_rep, d_ln_gain, d_ln_bias, d_w_in, d_w_out, d_w_pde)
```

```python
import functools

import jax
import jax.numpy as jnp
from jax import lax
from jax.experimental import pallas as pl
from jax.experimental.pallas import tpu as pltpu
from jax.sharding import PartitionSpec as P

epsilon = 1e-05
MESH = pl.DeviceIdType.MESH
HI = lax.Precision.HIGHEST


def mm(a, b, dims):
    return lax.dot_general(a, b, (dims, ((), ())), precision=HI, preferred_element_type=jnp.float32)


def dot_nn(a, b):
    return mm(a, b, ((1,), (0,)))


def dot_nt(a, b):
    return mm(a, b, ((1,), (1,)))


def dot_tn(a, b):
    return mm(a, b, ((0,), (0,)))


def remote(src, dst, sends, recvs, slot, device):
    return pltpu.make_async_remote_copy(
        src_ref=src,
        dst_ref=dst,
        send_sem=sends.at[slot],
        recv_sem=recvs.at[slot],
        device_id=device,
        device_id_type=MESH,
    )


def spread(values, tile_rows, tile_cols):
    pairs = tile_rows * tile_cols
    rows = jnp.broadcast_to(values[:, None, :], (tile_rows, tile_cols, tile_cols))
    rows = rows.reshape(pairs, tile_cols)
    place = lax.broadcasted_iota(jnp.int32, (pairs, tile_cols), 0) % tile_cols
    lane = lax.broadcasted_iota(jnp.int32, (pairs, tile_cols), 1)
    return jnp.sum(jnp.where(place == lane, rows, 0.0), axis=1, keepdims=True)


def kernel(
    sizes,
    x_ref, gain_ref, bias_ref, win_ref, wout_ref, wpde_ref, lab_ref, mask_ref,
    loss_out, dx_out, gain_out, bias_out, din_out, dout_out, pde_out,
    pair_send, pair_recv,
    small, small_core, small_row, small_z, small_last,
    norm, norm_core, norm_row, norm_z,
    go, go_core, go_row, go_sum, go_z,
    gi, gi_core, gi_row, gi_sum, gi_z,
    pair_ss, pair_rs, core_ss, core_rs, row_ss, row_rs, z_ss, z_rs, last_ss, last_rs,
):
    R, Z, tile_rows, tile_cols, bins, nb = sizes
    factor = tile_rows // tile_cols
    slab = tile_cols * tile_cols
    pairs = tile_rows * tile_cols
    r = lax.axis_index("row")
    c = lax.axis_index("col")
    core = c % 2
    z = c // 2
    sibling = z * 2 + 1 - core
    mirror_row = c // factor
    mirror_slab = c % factor
    channels = x_ref.shape[1]
    hidden_units = wout_ref.shape[0]

    barrier = pltpu.get_barrier_semaphore()

    def greet(row, col):
        pl.semaphore_signal(barrier, inc=1, device_id=(row, col), device_id_type=MESH)

    for k in range(factor):
        partner_col = r * factor + k

        @pl.when(jnp.logical_or(mirror_row != r, partner_col != c))
        def _():
            greet(mirror_row, partner_col)

    greet(r, sibling)
    for d in range(1, R):
        greet((r + d) % R, c)
        greet((r + d) % R, sibling)
    for e in range(1, Z):
        greet(r, ((z + e) % Z) * 2 + core)
    greeted = factor + 1 + 2 * (R - 1) + (Z - 1)

    x = x_ref[...]
    gain = gain_ref[...]
    average = jnp.mean(x, axis=-1, keepdims=True)
    centred = x - average
    variance = jnp.mean(centred * centred, axis=-1, keepdims=True)
    rstd = lax.rsqrt(variance + epsilon)
    xhat = centred * rstd
    normed = xhat * gain + bias_ref[...]
    gate = dot_nt(normed, win_ref[:hidden_units, :])
    up = dot_nt(normed, win_ref[hidden_units:, :])
    sig = 1.0 / (1.0 + jnp.exp(-gate))
    silu = gate * sig
    hidden = silu * up
    updated = x + dot_nn(hidden, wout_ref[...])
    w_pde = wpde_ref[...]
    projected = dot_nn(updated, w_pde)
    label = spread(lab_ref[...].astype(jnp.float32), tile_rows, tile_cols)
    mask = spread(mask_ref[...].astype(jnp.float32), tile_rows, tile_cols)
    bin_index = lax.broadcasted_iota(jnp.int32, (pairs, bins), 1).astype(jnp.float32)
    onehot = (bin_index == label).astype(jnp.float32)
    both = jnp.concatenate([projected, onehot], axis=1)
    pair_send[...] = both.reshape(factor, tile_cols, tile_cols, 2 * bins)

    @pl.when(mirror_row == r)
    def _():
        pl.semaphore_wait(barrier, greeted - 1)

    @pl.when(mirror_row != r)
    def _():
        pl.semaphore_wait(barrier, greeted)

    def pair_each(k, act, own):
        alone = jnp.logical_and(mirror_row == r, r * factor + k == c)

        @pl.when(jnp.logical_not(alone))
        def _():
            act(k)

        if own is not None:
            @pl.when(alone)
            def _():
                own(k)

    def start_pair(k):
        pltpu.make_async_remote_copy(
            src_ref=pair_send.at[k],
            dst_ref=pair_recv.at[mirror_slab],
            send_sem=pair_ss.at[k],
            recv_sem=pair_rs.at[mirror_slab],
            device_id=(mirror_row, r * factor + k),
            device_id_type=MESH,
        ).start()

    def own_pair(k):
        pair_recv[k] = pair_send[k]

    def wait_pair(k):
        taken = pltpu.make_async_remote_copy(
            src_ref=pair_send.at[k],
            dst_ref=pair_recv.at[k],
            send_sem=pair_ss.at[k],
            recv_sem=pair_rs.at[k],
            device_id=(mirror_row, r * factor + k),
            device_id_type=MESH,
        )
        taken.wait_recv()
        taken.wait_send()

    for k in range(factor):
        pair_each(k, start_pair, own_pair)
    for k in range(factor):
        pair_each(k, wait_pair, None)

    mirrored = jnp.concatenate(
        [
            jnp.concatenate([pair_recv[k, :, i, :] for i in range(tile_cols)], axis=0)
            for k in range(factor)
        ],
        axis=0,
    )
    total = both + mirrored
    scores = total[:, :bins]
    highest = jnp.max(scores, axis=-1, keepdims=True)
    shifted = jnp.exp(scores - highest)
    exp_total = jnp.sum(shifted, axis=-1, keepdims=True)
    log_total = highest + jnp.log(exp_total)
    picked = jnp.sum(scores * onehot, axis=-1, keepdims=True)
    loss = jnp.sum(mask * (log_total - picked))
    count = jnp.sum(mask)
    d_sym = mask * (2.0 * (shifted / exp_total) - total[:, bins:])

    def core_copy(wave, src, dst):
        return remote(src, dst, core_ss, core_rs, wave, (r, sibling))

    def row_copies(wave, src, dst):
        return [
            remote(src((r + d) % R), dst.at[r], row_ss, row_rs, wave * (R - 1) + d - 1, ((r + d) % R, c))
            for d in range(1, R)
        ]

    def z_copies(wave, src, dst):
        return [
            remote(
                src((z + e) % Z), dst.at[z], z_ss, z_rs, wave * (Z - 1) + e - 1, (r, ((z + e) % Z) * 2 + core)
            )
            for e in range(1, Z)
        ]

    def start(copies):
        for copy in copies:
            copy.start()

    def finish(copies):
        for copy in copies:
            copy.wait()

    def add_up(ref, count):
        value = ref[0]
        for s in range(1, count):
            value = value + ref[s]
        return value

    pde_t = dot_tn(d_sym, updated)
    top = small.shape[2] - 8
    row_index = lax.broadcasted_iota(jnp.int32, (8, channels), 0)
    meta = jnp.where(row_index == 0, loss, jnp.where(row_index == 1, count, 0.0))
    for a in range(2):
        for b in range(R):
            q = a * R + b
            small[a, b, :nb, :] = pde_t[q * nb:(q + 1) * nb, :]
            small[a, b, top:, :] = meta
    small_c = core_copy(0, small.at[1 - core], small_core)
    small_c.start()

    d_updated = dot_nt(d_sym, w_pde)
    go[...] = dot_tn(hidden, d_updated).reshape(go.shape)
    go_c = core_copy(1, go.at[:, :, 1 - core], go_core)
    go_c.start()

    d_hidden = dot_nt(d_updated, wout_ref[...])

    small_c.wait()
    small_core[...] = small_core[...] + small[core]
    small_row[r] = small_core[r]
    small_r = row_copies(0, lambda s: small_core.at[s], small_row)
    start(small_r)

    d_up = d_hidden * silu
    d_gate = d_hidden * up * (sig * (1.0 + gate * (1.0 - sig)))
    d_proj = jnp.concatenate([d_gate, d_up], axis=1)
    gi[...] = dot_tn(d_proj, normed).reshape(gi.shape)
    gi_c = core_copy(2, gi.at[:, :, 1 - core], gi_core)

    go_c.wait()
    gi_c.start()
    go_core[...] = go_core[...] + go[:, :, core]
    go_row[r] = go_core[r]
    go_r = row_copies(1, lambda s: go_core.at[s], go_row)
    start(go_r)

    d_normed = dot_nn(d_proj, win_ref[...])
    d_gain = jnp.sum(d_normed * xhat, axis=0, keepdims=True)
    d_bias = jnp.sum(d_normed, axis=0, keepdims=True)
    norm[...] = jnp.where(row_index == 0, d_gain, jnp.where(row_index == 1, d_bias, 0.0))
    norm_c = core_copy(3, norm, norm_core)
    norm_c.start()

    finish(small_r)
    small_z[z] = add_up(small_row, R)
    small_zc = z_copies(0, lambda s: small_z.at[z], small_z)
    start(small_zc)

    d_xhat = d_normed * gain
    first = jnp.mean(d_xhat, axis=-1, keepdims=True)
    second = jnp.mean(d_xhat * xhat, axis=-1, keepdims=True)
    dx = rstd * (d_xhat - first - xhat * second) + d_updated

    gi_c.wait()
    gi_core[...] = gi_core[...] + gi[:, :, core]
    gi_row[r] = gi_core[r]
    gi_r = row_copies(2, lambda s: gi_core.at[s], gi_row)
    start(gi_r)

    norm_c.wait()
    norm_core[...] = norm_core[...] + norm[...]
    norm_row[r] = norm_core[...]
    norm_r = row_copies(3, lambda s: norm_core, norm_row)
    start(norm_r)

    finish(go_r)
    go_sum[...] = add_up(go_row, R)
    go_zc = z_copies(1, lambda s: go_sum.at[s], go_z)
    start(go_zc)
    go_z[z] = go_sum[z]

    finish(small_zc)
    reduced = add_up(small_z, Z)
    whole_count = reduced[top + 1:top + 2, :]
    inverse = 1.0 / whole_count
    loss_out[...] = (reduced[top:top + 1, :] * inverse)[:, :1]
    mine = core * R + r
    small_last[mine] = reduced[:top]
    last = []
    for a in range(2):
        for d in range(R):
            if a or d:
                where = ((r + d) % R, z * 2 + (core + a) % 2)
                last.append(
                    remote(small_last.at[mine], small_last.at[mine], last_ss, last_rs, a * R + d - 1, where)
                )
    start(last)
    dx_out[...] = dx * inverse

    finish(gi_r)
    gi_sum[...] = add_up(gi_row, R)
    gi_zc = z_copies(2, lambda s: gi_sum.at[s], gi_z)
    start(gi_zc)
    gi_z[z] = gi_sum[z]
    finish(norm_r)
    norm_z[z] = add_up(norm_row, R)
    norm_zc = z_copies(3, lambda s: norm_z.at[z], norm_z)
    start(norm_zc)

    finish(go_zc)
    dout_out[...] = add_up(go_z, Z) * inverse
    finish(last)
    for q in range(2 * R):
        pde_out[q * nb:(q + 1) * nb, :] = small_last[q, :nb, :] * inverse
    finish(gi_zc)
    din_out[...] = add_up(gi_z, Z) * inverse
    finish(norm_zc)
    norm_all = add_up(norm_z, Z) * inverse
    gain_out[...] = norm_all[0:1]
    bias_out[...] = norm_all[1:2]


def on_device(pair_rep, ln_gain, ln_bias, w_in, w_out, w_pde, labels, pair_mask):
    tile_rows, tile_cols, channels = pair_rep.shape
    bins = w_pde.shape[1]
    R = lax.axis_size("row")
    Z = lax.axis_size("col") // 2
    owners = R * Z * 2
    pairs = tile_rows * tile_cols
    factor = tile_rows // tile_cols
    nb = bins // (2 * R)
    nbp = -(-nb // 8) * 8
    rows_i = w_in.shape[0] // owners
    rows_o = w_out.shape[0] // owners
    f32 = jnp.float32

    def vmem(*shape):
        return pltpu.VMEM(shape, f32)

    def wave(rows):
        return [
            vmem(R, Z, 2, rows, channels),
            vmem(R, Z, rows, channels),
            vmem(R, Z, rows, channels),
            vmem(Z, rows, channels),
            vmem(Z, rows, channels),
        ]

    dma = pltpu.SemaphoreType.DMA
    pair_send_shape = (factor, tile_cols, tile_cols, 2 * bins)
    scratch = [
        vmem(*pair_send_shape),
        vmem(*pair_send_shape),
        vmem(2, R, nbp + 8, channels),
        vmem(R, nbp + 8, channels),
        vmem(R, nbp + 8, channels),
        vmem(Z, nbp + 8, channels),
        vmem(2 * R, nbp, channels),
        vmem(8, channels),
        vmem(8, channels),
        vmem(R, 8, channels),
        vmem(Z, 8, channels),
        *wave(rows_o),
        *wave(rows_i),
        dma((factor,)),
        dma((factor,)),
        dma((4,)),
        dma((4,)),
        dma((4 * (R - 1),)),
        dma((4 * (R - 1),)),
        dma((4 * (Z - 1),)),
        dma((4 * (Z - 1),)),
        dma((2 * R - 1,)),
        dma((2 * R - 1,)),
    ]
    shape = jax.ShapeDtypeStruct
    loss, dx, gain, bias, d_in, d_out, pde_t = pl.pallas_call(
        functools.partial(kernel, (R, Z, tile_rows, tile_cols, bins, nb)),
        out_shape=[
            shape((1, 1), f32),
            shape((pairs, channels), f32),
            shape((1, channels), f32),
            shape((1, channels), f32),
            shape((rows_i, channels), f32),
            shape((rows_o, channels), f32),
            shape((bins, channels), f32),
        ],
        in_specs=[pl.BlockSpec(memory_space=pltpu.VMEM)] * 8,
        out_specs=[pl.BlockSpec(memory_space=pltpu.VMEM)] * 7,
        scratch_shapes=scratch,
        compiler_params=pltpu.CompilerParams(collective_id=0, has_side_effects=True),
        name="head_step",
    )(
        pair_rep.reshape(pairs, channels),
        ln_gain.reshape(1, channels),
        ln_bias.reshape(1, channels),
        w_in,
        w_out,
        w_pde,
        labels,
        pair_mask,
    )
    return (
        loss.reshape(()),
        dx.reshape(pair_rep.shape),
        gain.reshape(channels),
        bias.reshape(channels),
        d_in,
        d_out,
        pde_t.T,
    )


def solution(mesh):
    placed = (P("row", "col", None), P(), P(), P(), P(), P(), P("row", "col"), P("row", "col"))
    return jax.shard_map(
        on_device,
        mesh=mesh,
        in_specs=placed,
        out_specs=(
            P(),
            P("row", "col", None),
            P(),
            P(),
            P(("row", "col"), None),
            P(("row", "col"), None),
            P(),
        ),
        check_vma=False,
    )
```

```python
import functools

import jax
import jax.numpy as jnp
from jax import lax
from jax.experimental import pallas as pl
from jax.experimental.pallas import tpu as pltpu
from jax.sharding import PartitionSpec as P

epsilon = 1e-05
MESH = pl.DeviceIdType.MESH
HI = lax.Precision.HIGHEST


def mm(a, b, dims):
    return lax.dot_general(a, b, (dims, ((), ())), precision=HI, preferred_element_type=jnp.float32)


def dot_nn(a, b):
    return mm(a, b, ((1,), (0,)))


def dot_nt(a, b):
    return mm(a, b, ((1,), (1,)))


def dot_tn(a, b):
    return mm(a, b, ((0,), (0,)))


def remote(src, dst, sends, recvs, slot, device):
    return pltpu.make_async_remote_copy(
        src_ref=src,
        dst_ref=dst,
        send_sem=sends.at[slot],
        recv_sem=recvs.at[slot],
        device_id=device,
        device_id_type=MESH,
    )


def spread(values, tile_rows, tile_cols):
    pairs = tile_rows * tile_cols
    values = values.T
    rows = jnp.broadcast_to(values[:, None, :], (tile_rows, tile_cols, tile_cols))
    rows = rows.reshape(pairs, tile_cols)
    place = lax.broadcasted_iota(jnp.int32, (pairs, tile_cols), 0) % tile_cols
    lane = lax.broadcasted_iota(jnp.int32, (pairs, tile_cols), 1)
    return jnp.sum(jnp.where(place == lane, rows, 0.0), axis=1, keepdims=True)


def kernel(
    sizes,
    x_ref, gain_ref, bias_ref, win_ref, wout_ref, wpde_ref, lab_ref, mask_ref,
    loss_out, dx_out, gain_out, bias_out, din_out, dout_out, pde_out,
    pair_send, pair_recv,
    small, small_core, small_row, small_z, small_last,
    norm, norm_core, norm_row, norm_z,
    go, go_core, go_row, go_sum, go_z,
    gi, gi_core, gi_row, gi_sum, gi_z,
    pair_ss, pair_rs, core_ss, core_rs, row_ss, row_rs, z_ss, z_rs, last_ss, last_rs,
):
    R, Z, tile_rows, tile_cols, bins, nb = sizes
    factor = tile_rows // tile_cols
    slab = tile_cols * tile_cols
    pairs = tile_rows * tile_cols
    r = lax.axis_index("row")
    c = lax.axis_index("col")
    core = c % 2
    z = c // 2
    sibling = z * 2 + 1 - core
    mirror_row = c // factor
    mirror_slab = c % factor
    channels = x_ref.shape[1]
    hidden_units = wout_ref.shape[0]

    barrier = pltpu.get_barrier_semaphore()

    def greet(row, col):
        pl.semaphore_signal(barrier, inc=1, device_id=(row, col), device_id_type=MESH)

    for k in range(factor):
        partner_col = r * factor + k

        @pl.when(jnp.logical_or(mirror_row != r, partner_col != c))
        def _():
            greet(mirror_row, partner_col)

    greet(r, sibling)
    for d in range(1, R):
        greet((r + d) % R, c)
        greet((r + d) % R, sibling)
    for e in range(1, Z):
        greet(r, ((z + e) % Z) * 2 + core)
    greeted = factor + 1 + 2 * (R - 1) + (Z - 1)

    x = x_ref[...]
    gain = gain_ref[...]
    average = jnp.mean(x, axis=-1, keepdims=True)
    centred = x - average
    variance = jnp.mean(centred * centred, axis=-1, keepdims=True)
    rstd = lax.rsqrt(variance + epsilon)
    xhat = centred * rstd
    normed = xhat * gain + bias_ref[...]
    gate = dot_nt(normed, win_ref[:hidden_units, :])
    up = dot_nt(normed, win_ref[hidden_units:, :])
    sig = 1.0 / (1.0 + jnp.exp(-gate))
    silu = gate * sig
    hidden = silu * up
    updated = x + dot_nn(hidden, wout_ref[...])
    w_pde = wpde_ref[...]
    projected = dot_nt(updated, w_pde)
    label = spread(lab_ref[...].astype(jnp.float32), tile_rows, tile_cols)
    mask = spread(mask_ref[...].astype(jnp.float32), tile_rows, tile_cols)
    bin_index = lax.broadcasted_iota(jnp.int32, (pairs, bins), 1).astype(jnp.float32)
    onehot = (bin_index == label).astype(jnp.float32)
    both = jnp.concatenate([projected, onehot], axis=1)
    pair_send[...] = both.reshape(factor, tile_cols, tile_cols, 2 * bins)

    @pl.when(mirror_row == r)
    def _():
        pl.semaphore_wait(barrier, greeted - 1)

    @pl.when(mirror_row != r)
    def _():
        pl.semaphore_wait(barrier, greeted)

    def pair_each(k, act, own):
        alone = jnp.logical_and(mirror_row == r, r * factor + k == c)

        @pl.when(jnp.logical_not(alone))
        def _():
            act(k)

        if own is not None:
            @pl.when(alone)
            def _():
                own(k)

    def start_pair(k):
        pltpu.make_async_remote_copy(
            src_ref=pair_send.at[k],
            dst_ref=pair_recv.at[mirror_slab],
            send_sem=pair_ss.at[k],
            recv_sem=pair_rs.at[mirror_slab],
            device_id=(mirror_row, r * factor + k),
            device_id_type=MESH,
        ).start()

    def own_pair(k):
        pair_recv[k] = pair_send[k]

    def wait_pair(k):
        taken = pltpu.make_async_remote_copy(
            src_ref=pair_send.at[k],
            dst_ref=pair_recv.at[k],
            send_sem=pair_ss.at[k],
            recv_sem=pair_rs.at[k],
            device_id=(mirror_row, r * factor + k),
            device_id_type=MESH,
        )
        taken.wait_recv()
        taken.wait_send()

    for k in range(factor):
        pair_each(k, start_pair, own_pair)
    for k in range(factor):
        pair_each(k, wait_pair, None)

    mirrored = jnp.concatenate(
        [
            jnp.concatenate([pair_recv[k, :, i, :] for i in range(tile_cols)], axis=0)
            for k in range(factor)
        ],
        axis=0,
    )
    total = both + mirrored
    scores = total[:, :bins]
    highest = jnp.max(scores, axis=-1, keepdims=True)
    shifted = jnp.exp(scores - highest)
    exp_total = jnp.sum(shifted, axis=-1, keepdims=True)
    log_total = highest + jnp.log(exp_total)
    picked = jnp.sum(scores * onehot, axis=-1, keepdims=True)
    loss = jnp.sum(mask * (log_total - picked))
    count = jnp.sum(mask)
    d_sym = mask * (2.0 * (shifted / exp_total) - total[:, bins:])

    def core_copy(wave, src, dst):
        return remote(src, dst, core_ss, core_rs, wave, (r, sibling))

    def row_copies(wave, src, dst):
        return [
            remote(src((r + d) % R), dst.at[r], row_ss, row_rs, wave * (R - 1) + d - 1, ((r + d) % R, c))
            for d in range(1, R)
        ]

    def z_copies(wave, src, dst):
        return [
            remote(
                src((z + e) % Z), dst.at[z], z_ss, z_rs, wave * (Z - 1) + e - 1, (r, ((z + e) % Z) * 2 + core)
            )
            for e in range(1, Z)
        ]

    def start(copies):
        for copy in copies:
            copy.start()

    def finish(copies):
        for copy in copies:
            copy.wait()

    def add_up(ref, count):
        value = ref[0]
        for s in range(1, count):
            value = value + ref[s]
        return value

    pde_t = dot_tn(d_sym, updated)
    top = small.shape[2] - 8
    row_index = lax.broadcasted_iota(jnp.int32, (8, channels), 0)
    meta = jnp.where(row_index == 0, loss, jnp.where(row_index == 1, count, 0.0))
    for a in range(2):
        for b in range(R):
            q = a * R + b
            small[a, b, :nb, :] = pde_t[q * nb:(q + 1) * nb, :]
            small[a, b, top:, :] = meta
    small_c = core_copy(0, small.at[1 - core], small_core)
    small_c.start()

    d_updated = dot_nn(d_sym, w_pde)
    go[...] = dot_tn(hidden, d_updated).reshape(go.shape)
    go_c = core_copy(1, go.at[:, :, 1 - core], go_core)
    go_c.start()

    d_hidden = dot_nt(d_updated, wout_ref[...])

    small_c.wait()
    small_core[...] = small_core[...] + small[core]
    small_row[r] = small_core[r]
    small_r = row_copies(0, lambda s: small_core.at[s], small_row)
    start(small_r)

    d_up = d_hidden * silu
    d_gate = d_hidden * up * (sig * (1.0 + gate * (1.0 - sig)))
    d_proj = jnp.concatenate([d_gate, d_up], axis=1)
    gi[...] = dot_tn(d_proj, normed).reshape(gi.shape)
    gi_c = core_copy(2, gi.at[:, :, 1 - core], gi_core)

    go_c.wait()
    gi_c.start()
    go_core[...] = go_core[...] + go[:, :, core]
    go_row[r] = go_core[r]
    go_r = row_copies(1, lambda s: go_core.at[s], go_row)
    start(go_r)

    d_normed = dot_nn(d_proj, win_ref[...])
    d_gain = jnp.sum(d_normed * xhat, axis=0, keepdims=True)
    d_bias = jnp.sum(d_normed, axis=0, keepdims=True)
    norm[...] = jnp.where(row_index == 0, d_gain, jnp.where(row_index == 1, d_bias, 0.0))
    norm_c = core_copy(3, norm, norm_core)
    norm_c.start()

    finish(small_r)
    small_z[z] = add_up(small_row, R)
    small_zc = z_copies(0, lambda s: small_z.at[z], small_z)
    start(small_zc)

    d_xhat = d_normed * gain
    first = jnp.mean(d_xhat, axis=-1, keepdims=True)
    second = jnp.mean(d_xhat * xhat, axis=-1, keepdims=True)
    dx = rstd * (d_xhat - first - xhat * second) + d_updated

    gi_c.wait()
    gi_core[...] = gi_core[...] + gi[:, :, core]
    gi_row[r] = gi_core[r]
    gi_r = row_copies(2, lambda s: gi_core.at[s], gi_row)
    start(gi_r)

    norm_c.wait()
    norm_core[...] = norm_core[...] + norm[...]
    norm_row[r] = norm_core[...]
    norm_r = row_copies(3, lambda s: norm_core, norm_row)
    start(norm_r)

    finish(go_r)
    go_sum[...] = add_up(go_row, R)
    go_zc = z_copies(1, lambda s: go_sum.at[s], go_z)
    start(go_zc)
    go_z[z] = go_sum[z]

    finish(small_zc)
    reduced = add_up(small_z, Z)
    whole_count = reduced[top + 1:top + 2, :]
    inverse = 1.0 / whole_count
    loss_out[...] = (reduced[top:top + 1, :] * inverse)[:, :1]
    mine = core * R + r
    small_last[mine] = reduced[:top]
    last = []
    for a in range(2):
        for d in range(R):
            if a or d:
                where = ((r + d) % R, z * 2 + (core + a) % 2)
                last.append(
                    remote(small_last.at[mine], small_last.at[mine], last_ss, last_rs, a * R + d - 1, where)
                )
    start(last)
    dx_out[...] = dx * inverse

    finish(gi_r)
    gi_sum[...] = add_up(gi_row, R)
    gi_zc = z_copies(2, lambda s: gi_sum.at[s], gi_z)
    start(gi_zc)
    gi_z[z] = gi_sum[z]
    finish(norm_r)
    norm_z[z] = add_up(norm_row, R)
    norm_zc = z_copies(3, lambda s: norm_z.at[z], norm_z)
    start(norm_zc)

    finish(go_zc)
    dout_out[...] = add_up(go_z, Z) * inverse
    finish(last)
    for q in range(2 * R):
        pde_out[q * nb:(q + 1) * nb, :] = small_last[q, :nb, :] * inverse
    finish(gi_zc)
    din_out[...] = add_up(gi_z, Z) * inverse
    finish(norm_zc)
    norm_all = add_up(norm_z, Z) * inverse
    gain_out[...] = norm_all[0:1]
    bias_out[...] = norm_all[1:2]


def put_out(*refs):
    sems = refs[-1]
    half = (len(refs) - 1) // 2
    copies = [
        pltpu.make_async_copy(refs[k], refs[half + k], sems.at[k]) for k in range(half)
    ]
    for copy in copies:
        copy.start()
    for copy in copies:
        copy.wait()


def on_device(pair_rep, ln_gain, ln_bias, w_in, w_out, w_pde, labels, pair_mask):
    tile_rows, tile_cols, channels = pair_rep.shape
    bins = w_pde.shape[1]
    R = lax.axis_size("row")
    Z = lax.axis_size("col") // 2
    owners = R * Z * 2
    pairs = tile_rows * tile_cols
    factor = tile_rows // tile_cols
    nb = bins // (2 * R)
    nbp = -(-nb // 8) * 8
    rows_i = w_in.shape[0] // owners
    rows_o = w_out.shape[0] // owners
    f32 = jnp.float32

    def vmem(*shape):
        return pltpu.VMEM(shape, f32)

    def wave(rows):
        return [
            vmem(R, Z, 2, rows, channels),
            vmem(R, Z, rows, channels),
            vmem(R, Z, rows, channels),
            vmem(Z, rows, channels),
            vmem(Z, rows, channels),
        ]

    dma = pltpu.SemaphoreType.DMA
    pair_send_shape = (factor, tile_cols, tile_cols, 2 * bins)
    scratch = [
        vmem(*pair_send_shape),
        vmem(*pair_send_shape),
        vmem(2, R, nbp + 8, channels),
        vmem(R, nbp + 8, channels),
        vmem(R, nbp + 8, channels),
        vmem(Z, nbp + 8, channels),
        vmem(2 * R, nbp, channels),
        vmem(8, channels),
        vmem(8, channels),
        vmem(R, 8, channels),
        vmem(Z, 8, channels),
        *wave(rows_o),
        *wave(rows_i),
        dma((factor,)),
        dma((factor,)),
        dma((4,)),
        dma((4,)),
        dma((4 * (R - 1),)),
        dma((4 * (R - 1),)),
        dma((4 * (Z - 1),)),
        dma((4 * (Z - 1),)),
        dma((2 * R - 1,)),
        dma((2 * R - 1,)),
    ]
    shape = jax.ShapeDtypeStruct
    held = pl.pallas_call(
        functools.partial(kernel, (R, Z, tile_rows, tile_cols, bins, nb)),
        out_shape=[
            vmem(1, 1),
            vmem(pairs, channels),
            vmem(1, channels),
            vmem(1, channels),
            vmem(rows_i, channels),
            vmem(rows_o, channels),
            vmem(bins, channels),
        ],
        in_specs=[pl.BlockSpec(memory_space=pltpu.VMEM)] * 8,
        out_specs=[pl.BlockSpec(memory_space=pltpu.VMEM)] * 7,
        scratch_shapes=scratch,
        compiler_params=pltpu.CompilerParams(collective_id=0, has_side_effects=True),
        name="head_step",
    )(
        pair_rep.reshape(pairs, channels),
        ln_gain.reshape(1, channels),
        ln_bias.reshape(1, channels),
        w_in,
        w_out,
        w_pde.T,
        labels.T,
        pair_mask.T,
    )
    held = [pltpu.with_memory_space_constraint(value, pltpu.VMEM) for value in held]
    loss, dx, gain, bias, d_in, d_out, pde_t = pl.pallas_call(
        put_out,
        out_shape=[shape(value.shape, f32) for value in held],
        in_specs=[pl.BlockSpec(memory_space=pltpu.VMEM)] * 7,
        out_specs=[pl.BlockSpec(memory_space=pl.ANY)] * 7,
        scratch_shapes=[dma((7,))],
        name="put_out",
    )(*held)
    return (
        loss.reshape(()),
        dx.reshape(pair_rep.shape),
        gain.reshape(channels),
        bias.reshape(channels),
        d_in,
        d_out,
        pde_t.T,
    )


def solution(mesh):
    placed = (P("row", "col", None), P(), P(), P(), P(), P(), P("row", "col"), P("row", "col"))
    return jax.shard_map(
        on_device,
        mesh=mesh,
        in_specs=placed,
        out_specs=(
            P(),
            P("row", "col", None),
            P(),
            P(),
            P(("row", "col"), None),
            P(("row", "col"), None),
            P(),
        ),
        check_vma=False,
    )
```

```python
import functools

import jax
import jax.numpy as jnp
from jax import lax
from jax.experimental import pallas as pl
from jax.experimental.pallas import tpu as pltpu
from jax.sharding import PartitionSpec as P

epsilon = 1e-05
MESH = pl.DeviceIdType.MESH
HI = lax.Precision.HIGHEST


def mm(a, b, dims):
    return lax.dot_general(a, b, (dims, ((), ())), precision=HI, preferred_element_type=jnp.float32)


def dot_nn(a, b):
    return mm(a, b, ((1,), (0,)))


def dot_nt(a, b):
    return mm(a, b, ((1,), (1,)))


def dot_tn(a, b):
    return mm(a, b, ((0,), (0,)))


def remote(src, dst, sends, recvs, slot, device):
    return pltpu.make_async_remote_copy(
        src_ref=src,
        dst_ref=dst,
        send_sem=sends.at[slot],
        recv_sem=recvs.at[slot],
        device_id=device,
        device_id_type=MESH,
    )


def spread(values, tile_rows, tile_cols):
    pairs = tile_rows * tile_cols
    values = values.T
    rows = jnp.broadcast_to(values[:, None, :], (tile_rows, tile_cols, tile_cols))
    rows = rows.reshape(pairs, tile_cols)
    place = lax.broadcasted_iota(jnp.int32, (pairs, tile_cols), 0) % tile_cols
    lane = lax.broadcasted_iota(jnp.int32, (pairs, tile_cols), 1)
    return jnp.sum(jnp.where(place == lane, rows, 0.0), axis=1, keepdims=True)


def kernel(
    sizes,
    x_hbm, gain_hbm, bias_hbm, win_hbm, wout_hbm, wpde_hbm, lab_hbm, mask_hbm,
    loss_out, dx_out, gain_out, bias_out, din_out, dout_out, pde_out,
    pair_send, pair_recv,
    small, small_core, small_row, small_z, small_last,
    norm, norm_core, norm_row, norm_z,
    go, go_core, go_row, go_sum, go_z,
    ga, ga_core, ga_row, ga_sum, ga_z,
    gb, gb_core, gb_row, gb_sum, gb_z,
    x_ref, gain_ref, bias_ref, win_ref, wout_ref, wpde_ref, lab_ref, mask_ref, load_sems,
    pair_ss, pair_rs, core_ss, core_rs, row_ss, row_rs, z_ss, z_rs, last_ss, last_rs,
):
    R, Z, tile_rows, tile_cols, bins, nb = sizes
    factor = tile_rows // tile_cols
    slab = tile_cols * tile_cols
    pairs = tile_rows * tile_cols
    r = lax.axis_index("row")
    c = lax.axis_index("col")
    core = c % 2
    z = c // 2
    sibling = z * 2 + 1 - core
    mirror_row = c // factor
    mirror_slab = c % factor
    channels = x_hbm.shape[1]
    hidden_units = wout_hbm.shape[0]

    barrier = pltpu.get_barrier_semaphore()

    def greet(row, col):
        pl.semaphore_signal(barrier, inc=1, device_id=(row, col), device_id_type=MESH)

    for k in range(factor):
        partner_col = r * factor + k

        @pl.when(jnp.logical_or(mirror_row != r, partner_col != c))
        def _():
            greet(mirror_row, partner_col)

    greet(r, sibling)
    for d in range(1, R):
        greet((r + d) % R, c)
        greet((r + d) % R, sibling)
    for e in range(1, Z):
        greet(r, ((z + e) % Z) * 2 + core)
    greeted = factor + 1 + 2 * (R - 1) + (Z - 1)

    loads = [
        pltpu.make_async_copy(source, target, load_sems.at[k])
        for k, (source, target) in enumerate(
            (
                (x_hbm, x_ref), (gain_hbm, gain_ref), (bias_hbm, bias_ref), (win_hbm, win_ref),
                (wout_hbm, wout_ref), (wpde_hbm, wpde_ref), (lab_hbm, lab_ref), (mask_hbm, mask_ref),
            )
        )
    ]
    for load in loads:
        load.start()

    for load in loads[:3]:
        load.wait()
    x = x_ref[...]
    gain = gain_ref[...]
    average = jnp.mean(x, axis=-1, keepdims=True)
    centred = x - average
    variance = jnp.mean(centred * centred, axis=-1, keepdims=True)
    rstd = lax.rsqrt(variance + epsilon)
    xhat = centred * rstd
    normed = xhat * gain + bias_ref[...]
    loads[3].wait()
    gate = dot_nt(normed, win_ref[:hidden_units, :])
    up = dot_nt(normed, win_ref[hidden_units:, :])
    sig = 1.0 / (1.0 + jnp.exp(-gate))
    silu = gate * sig
    hidden = silu * up
    loads[4].wait()
    updated = x + dot_nn(hidden, wout_ref[...])
    for load in loads[5:]:
        load.wait()
    w_pde = wpde_ref[...]
    projected = dot_nt(updated, w_pde)
    label = spread(lab_ref[...].astype(jnp.float32), tile_rows, tile_cols)
    mask = spread(mask_ref[...].astype(jnp.float32), tile_rows, tile_cols)
    bin_index = lax.broadcasted_iota(jnp.int32, (pairs, bins), 1).astype(jnp.float32)
    onehot = (bin_index == label).astype(jnp.float32)
    both = jnp.concatenate([projected, onehot], axis=1)
    pair_send[...] = both.reshape(factor, tile_cols, tile_cols, 2 * bins)

    @pl.when(mirror_row == r)
    def _():
        pl.semaphore_wait(barrier, greeted - 1)

    @pl.when(mirror_row != r)
    def _():
        pl.semaphore_wait(barrier, greeted)

    def pair_each(k, act, own):
        alone = jnp.logical_and(mirror_row == r, r * factor + k == c)

        @pl.when(jnp.logical_not(alone))
        def _():
            act(k)

        if own is not None:
            @pl.when(alone)
            def _():
                own(k)

    def start_pair(k):
        pltpu.make_async_remote_copy(
            src_ref=pair_send.at[k],
            dst_ref=pair_recv.at[mirror_slab],
            send_sem=pair_ss.at[k],
            recv_sem=pair_rs.at[mirror_slab],
            device_id=(mirror_row, r * factor + k),
            device_id_type=MESH,
        ).start()

    def own_pair(k):
        pair_recv[k] = pair_send[k]

    def wait_pair(k):
        taken = pltpu.make_async_remote_copy(
            src_ref=pair_send.at[k],
            dst_ref=pair_recv.at[k],
            send_sem=pair_ss.at[k],
            recv_sem=pair_rs.at[k],
            device_id=(mirror_row, r * factor + k),
            device_id_type=MESH,
        )
        taken.wait_recv()
        taken.wait_send()

    for k in range(factor):
        pair_each(k, start_pair, own_pair)
    for k in range(factor):
        pair_each(k, wait_pair, None)

    mirrored = jnp.concatenate(
        [
            jnp.concatenate([pair_recv[k, :, i, :] for i in range(tile_cols)], axis=0)
            for k in range(factor)
        ],
        axis=0,
    )
    total = both + mirrored
    scores = total[:, :bins]
    highest = jnp.max(scores, axis=-1, keepdims=True)
    shifted = jnp.exp(scores - highest)
    exp_total = jnp.sum(shifted, axis=-1, keepdims=True)
    log_total = highest + jnp.log(exp_total)
    picked = jnp.sum(scores * onehot, axis=-1, keepdims=True)
    loss = jnp.sum(mask * (log_total - picked))
    count = jnp.sum(mask)
    d_sym = mask * (2.0 * (shifted / exp_total) - total[:, bins:])

    def core_copy(wave, src, dst):
        return remote(src, dst, core_ss, core_rs, wave, (r, sibling))

    def row_copies(wave, src, dst):
        return [
            remote(src((r + d) % R), dst.at[r], row_ss, row_rs, wave * (R - 1) + d - 1, ((r + d) % R, c))
            for d in range(1, R)
        ]

    def z_copies(wave, src, dst):
        return [
            remote(
                src((z + e) % Z), dst.at[z], z_ss, z_rs, wave * (Z - 1) + e - 1, (r, ((z + e) % Z) * 2 + core)
            )
            for e in range(1, Z)
        ]

    def start(copies):
        for copy in copies:
            copy.start()

    def finish(copies):
        for copy in copies:
            copy.wait()

    def add_up(ref, count):
        value = ref[0]
        for s in range(1, count):
            value = value + ref[s]
        return value

    pde_t = dot_tn(d_sym, updated)
    top = small.shape[2] - 8
    row_index = lax.broadcasted_iota(jnp.int32, (8, channels), 0)
    meta = jnp.where(row_index == 0, loss, jnp.where(row_index == 1, count, 0.0))
    for a in range(2):
        for b in range(R):
            q = a * R + b
            small[a, b, :nb, :] = pde_t[q * nb:(q + 1) * nb, :]
            small[a, b, top:, :] = meta
    small_c = core_copy(0, small.at[1 - core], small_core)
    small_c.start()

    d_updated = dot_nn(d_sym, w_pde)
    go[...] = dot_tn(hidden, d_updated).reshape(go.shape)
    go_c = core_copy(1, go.at[:, :, 1 - core], go_core)
    go_c.start()

    d_hidden = dot_nt(d_updated, wout_ref[...])
    small_c.wait()
    small_core[...] = small_core[...] + small[core]
    small_row[r] = small_core[r]
    small_r = row_copies(0, lambda s: small_core.at[s], small_row)
    start(small_r)

    d_up = d_hidden * silu
    d_gate = d_hidden * up * (sig * (1.0 + gate * (1.0 - sig)))
    d_proj = jnp.concatenate([d_gate, d_up], axis=1)
    half = ga.shape[3]
    d_w_in = dot_tn(d_proj, normed).reshape(R, Z, 2, 2, half, channels)
    ga[...] = d_w_in[:, :, :, 0]
    gb[...] = d_w_in[:, :, :, 1]
    ga_c = core_copy(2, ga.at[:, :, 1 - core], ga_core)
    ga_c.start()
    gb_c = core_copy(4, gb.at[:, :, 1 - core], gb_core)
    gb_c.start()

    def to_rows(wave, copy, own, got, across):
        copy.wait()
        got[...] = got[...] + own[:, :, core]
        copies = row_copies(wave, lambda s: got.at[s], across)
        start(copies)
        across[r] = got[r]
        return copies

    def to_z(wave, copies, across, kept, along):
        finish(copies)
        kept[...] = add_up(across, R)
        copies = z_copies(wave, lambda s: kept.at[s], along)
        start(copies)
        along[z] = kept[z]
        return copies

    go_r = to_rows(1, go_c, go, go_core, go_row)

    d_normed = dot_nn(d_proj, win_ref[...])
    d_gain = jnp.sum(d_normed * xhat, axis=0, keepdims=True)
    d_bias = jnp.sum(d_normed, axis=0, keepdims=True)
    norm[...] = jnp.where(row_index == 0, d_gain, jnp.where(row_index == 1, d_bias, 0.0))
    norm_c = core_copy(3, norm, norm_core)
    norm_c.start()

    ga_r = to_rows(2, ga_c, ga, ga_core, ga_row)
    gb_r = to_rows(4, gb_c, gb, gb_core, gb_row)

    norm_c.wait()
    norm_core[...] = norm_core[...] + norm[...]
    norm_row[r] = norm_core[...]
    norm_r = row_copies(3, lambda s: norm_core, norm_row)
    start(norm_r)

    d_xhat = d_normed * gain
    first = jnp.mean(d_xhat, axis=-1, keepdims=True)
    second = jnp.mean(d_xhat * xhat, axis=-1, keepdims=True)
    dx = rstd * (d_xhat - first - xhat * second) + d_updated

    finish(small_r)
    small_z[z] = add_up(small_row, R)
    small_zc = z_copies(0, lambda s: small_z.at[z], small_z)
    start(small_zc)
    go_zc = to_z(1, go_r, go_row, go_sum, go_z)
    finish(small_zc)
    reduced = add_up(small_z, Z)
    whole_count = reduced[top + 1:top + 2, :]
    inverse = 1.0 / whole_count
    mine = core * R + r
    small_last[mine] = reduced[:top]
    last = []
    for a in range(2):
        for d in range(R):
            if a or d:
                where = ((r + d) % R, z * 2 + (core + a) % 2)
                last.append(
                    remote(small_last.at[mine], small_last.at[mine], last_ss, last_rs, a * R + d - 1, where)
                )
    start(last)
    loss_out[...] = (reduced[top:top + 1, :] * inverse)[:, :1]
    dx_out[...] = dx * inverse

    ga_zc = to_z(2, ga_r, ga_row, ga_sum, ga_z)

    finish(norm_r)
    norm_z[z] = add_up(norm_row, R)
    norm_zc = z_copies(3, lambda s: norm_z.at[z], norm_z)
    start(norm_zc)

    gb_zc = to_z(4, gb_r, gb_row, gb_sum, gb_z)

    finish(go_zc)
    dout_out[...] = add_up(go_z, Z) * inverse
    finish(norm_zc)
    norm_all = add_up(norm_z, Z) * inverse
    gain_out[...] = norm_all[0:1]
    bias_out[...] = norm_all[1:2]
    finish(ga_zc)
    din_out[:half, :] = add_up(ga_z, Z) * inverse
    finish(gb_zc)
    din_out[half:, :] = add_up(gb_z, Z) * inverse
    finish(last)
    for q in range(2 * R):
        pde_out[q * nb:(q + 1) * nb, :] = small_last[q, :nb, :] * inverse


def put_out(*refs):
    sems = refs[-1]
    half = (len(refs) - 1) // 2
    copies = [
        pltpu.make_async_copy(refs[k], refs[half + k], sems.at[k]) for k in range(half)
    ]
    for copy in copies:
        copy.start()
    for copy in copies:
        copy.wait()


def on_device(pair_rep, ln_gain, ln_bias, w_in, w_out, w_pde, labels, pair_mask):
    tile_rows, tile_cols, channels = pair_rep.shape
    bins = w_pde.shape[1]
    R = lax.axis_size("row")
    Z = lax.axis_size("col") // 2
    owners = R * Z * 2
    pairs = tile_rows * tile_cols
    factor = tile_rows // tile_cols
    nb = bins // (2 * R)
    nbp = -(-nb // 8) * 8
    rows_i = w_in.shape[0] // owners
    rows_o = w_out.shape[0] // owners
    f32 = jnp.float32

    def vmem(*shape):
        return pltpu.VMEM(shape, f32)

    def wave(rows):
        return [
            vmem(R, Z, 2, rows, channels),
            vmem(R, Z, rows, channels),
            vmem(R, Z, rows, channels),
            vmem(Z, rows, channels),
            vmem(Z, rows, channels),
        ]

    dma = pltpu.SemaphoreType.DMA
    pair_send_shape = (factor, tile_cols, tile_cols, 2 * bins)
    scratch = [
        vmem(*pair_send_shape),
        vmem(*pair_send_shape),
        vmem(2, R, nbp + 8, channels),
        vmem(R, nbp + 8, channels),
        vmem(R, nbp + 8, channels),
        vmem(Z, nbp + 8, channels),
        vmem(2 * R, nbp, channels),
        vmem(8, channels),
        vmem(8, channels),
        vmem(R, 8, channels),
        vmem(Z, 8, channels),
        *wave(rows_o),
        *wave(rows_i // 2),
        *wave(rows_i // 2),
        vmem(pairs, channels),
        vmem(1, channels),
        vmem(1, channels),
        vmem(*w_in.shape),
        vmem(*w_out.shape),
        vmem(bins, channels),
        pltpu.VMEM((tile_cols, tile_rows), labels.dtype),
        pltpu.VMEM((tile_cols, tile_rows), pair_mask.dtype),
        dma((8,)),
        dma((factor,)),
        dma((factor,)),
        dma((5,)),
        dma((5,)),
        dma((5 * (R - 1),)),
        dma((5 * (R - 1),)),
        dma((5 * (Z - 1),)),
        dma((5 * (Z - 1),)),
        dma((2 * R - 1,)),
        dma((2 * R - 1,)),
    ]
    shape = jax.ShapeDtypeStruct
    held = pl.pallas_call(
        functools.partial(kernel, (R, Z, tile_rows, tile_cols, bins, nb)),
        out_shape=[
            vmem(1, 1),
            vmem(pairs, channels),
            vmem(1, channels),
            vmem(1, channels),
            vmem(rows_i, channels),
            vmem(rows_o, channels),
            vmem(bins, channels),
        ],
        in_specs=[pl.BlockSpec(memory_space=pl.ANY)] * 8,
        out_specs=[pl.BlockSpec(memory_space=pltpu.VMEM)] * 7,
        scratch_shapes=scratch,
        compiler_params=pltpu.CompilerParams(collective_id=0, has_side_effects=True),
        name="head_step",
    )(
        pair_rep.reshape(pairs, channels),
        ln_gain.reshape(1, channels),
        ln_bias.reshape(1, channels),
        w_in,
        w_out,
        w_pde.T,
        labels.T,
        pair_mask.T,
    )
    held = [pltpu.with_memory_space_constraint(value, pltpu.VMEM) for value in held]
    loss, dx, gain, bias, d_in, d_out, pde_t = pl.pallas_call(
        put_out,
        out_shape=[shape(value.shape, f32) for value in held],
        in_specs=[pl.BlockSpec(memory_space=pltpu.VMEM)] * 7,
        out_specs=[pl.BlockSpec(memory_space=pl.ANY)] * 7,
        scratch_shapes=[dma((7,))],
        name="put_out",
    )(*held)
    return (
        loss.reshape(()),
        dx.reshape(pair_rep.shape),
        gain.reshape(channels),
        bias.reshape(channels),
        d_in,
        d_out,
        pde_t.T,
    )


def solution(mesh):
    placed = (P("row", "col", None), P(), P(), P(), P(), P(), P("row", "col"), P("row", "col"))
    return jax.shard_map(
        on_device,
        mesh=mesh,
        in_specs=placed,
        out_specs=(
            P(),
            P("row", "col", None),
            P(),
            P(),
            P(("row", "col"), None),
            P(("row", "col"), None),
            P(),
        ),
        check_vma=False,
    )
```

```python
import functools

import jax
import jax.numpy as jnp
from jax import lax
from jax.experimental import pallas as pl
from jax.experimental.pallas import tpu as pltpu
from jax.sharding import PartitionSpec as P

epsilon = 1e-05
MESH = pl.DeviceIdType.MESH
HI = lax.Precision.HIGHEST


def mm(a, b, dims):
    return lax.dot_general(a, b, (dims, ((), ())), precision=HI, preferred_element_type=jnp.float32)


def dot_nn(a, b):
    return mm(a, b, ((1,), (0,)))


def dot_nt(a, b):
    return mm(a, b, ((1,), (1,)))


def dot_tn(a, b):
    return mm(a, b, ((0,), (0,)))


def two(value):
    high = value.astype(jnp.bfloat16)
    return high, (value - high.astype(jnp.float32)).astype(jnp.bfloat16)


def mm3(a, b, dims):
    a_high, a_low = two(a)
    b_high, b_low = two(b)

    def part(p, q):
        return lax.dot_general(p, q, (dims, ((), ())), preferred_element_type=jnp.float32)

    return part(a_high, b_high) + (part(a_high, b_low) + part(a_low, b_high))


def remote(src, dst, sends, recvs, slot, device):
    return pltpu.make_async_remote_copy(
        src_ref=src,
        dst_ref=dst,
        send_sem=sends.at[slot],
        recv_sem=recvs.at[slot],
        device_id=device,
        device_id_type=MESH,
    )


def spread(values, tile_rows, tile_cols):
    pairs = tile_rows * tile_cols
    values = values.T
    rows = jnp.broadcast_to(values[:, None, :], (tile_rows, tile_cols, tile_cols))
    rows = rows.reshape(pairs, tile_cols)
    place = lax.broadcasted_iota(jnp.int32, (pairs, tile_cols), 0) % tile_cols
    lane = lax.broadcasted_iota(jnp.int32, (pairs, tile_cols), 1)
    return jnp.sum(jnp.where(place == lane, rows, 0.0), axis=1, keepdims=True)


def kernel(
    sizes,
    x_hbm, gain_hbm, bias_hbm, win_hbm, wout_hbm, wpde_hbm, lab_hbm, mask_hbm,
    loss_out, dx_out, gain_out, bias_out, din_out, dout_out, pde_out,
    pair_send, pair_recv,
    small, small_core, small_row, small_z, small_last,
    norm, norm_core, norm_row, norm_z,
    go, go_core, go_row, go_sum, go_z,
    ga, ga_core, ga_row, ga_sum, ga_z,
    gb, gb_core, gb_row, gb_sum, gb_z,
    x_ref, gain_ref, bias_ref, win_ref, wout_ref, wpde_ref, lab_ref, mask_ref, load_sems,
    pair_ss, pair_rs, core_ss, core_rs, row_ss, row_rs, z_ss, z_rs, last_ss, last_rs,
):
    R, Z, tile_rows, tile_cols, bins, nb = sizes
    factor = tile_rows // tile_cols
    slab = tile_cols * tile_cols
    pairs = tile_rows * tile_cols
    r = lax.axis_index("row")
    c = lax.axis_index("col")
    core = c % 2
    z = c // 2
    sibling = z * 2 + 1 - core
    mirror_row = c // factor
    mirror_slab = c % factor
    channels = x_hbm.shape[1]
    hidden_units = wout_hbm.shape[0]

    barrier = pltpu.get_barrier_semaphore()

    def greet(row, col):
        pl.semaphore_signal(barrier, inc=1, device_id=(row, col), device_id_type=MESH)

    for k in range(factor):
        partner_col = r * factor + k

        @pl.when(jnp.logical_or(mirror_row != r, partner_col != c))
        def _():
            greet(mirror_row, partner_col)

    greet(r, sibling)
    for d in range(1, R):
        greet((r + d) % R, c)
        greet((r + d) % R, sibling)
    for e in range(1, Z):
        greet(r, ((z + e) % Z) * 2 + core)
    greeted = factor + 1 + 2 * (R - 1) + (Z - 1)

    loads = [
        pltpu.make_async_copy(source, target, load_sems.at[k])
        for k, (source, target) in enumerate(
            (
                (x_hbm, x_ref), (gain_hbm, gain_ref), (bias_hbm, bias_ref), (win_hbm, win_ref),
                (wout_hbm, wout_ref), (wpde_hbm, wpde_ref), (lab_hbm, lab_ref), (mask_hbm, mask_ref),
            )
        )
    ]
    for load in loads:
        load.start()

    for load in loads[:3]:
        load.wait()
    x = x_ref[...]
    gain = gain_ref[...]
    average = jnp.mean(x, axis=-1, keepdims=True)
    centred = x - average
    variance = jnp.mean(centred * centred, axis=-1, keepdims=True)
    rstd = lax.rsqrt(variance + epsilon)
    xhat = centred * rstd
    normed = xhat * gain + bias_ref[...]
    loads[3].wait()
    gate = dot_nt(normed, win_ref[:hidden_units, :])
    up = dot_nt(normed, win_ref[hidden_units:, :])
    sig = 1.0 / (1.0 + jnp.exp(-gate))
    silu = gate * sig
    hidden = silu * up
    loads[4].wait()
    updated = x + dot_nn(hidden, wout_ref[...])
    for load in loads[5:]:
        load.wait()
    w_pde = wpde_ref[...]
    projected = dot_nt(updated, w_pde)
    label = spread(lab_ref[...].astype(jnp.float32), tile_rows, tile_cols)
    mask = spread(mask_ref[...].astype(jnp.float32), tile_rows, tile_cols)
    bin_index = lax.broadcasted_iota(jnp.int32, (pairs, bins), 1).astype(jnp.float32)
    onehot = (bin_index == label).astype(jnp.float32)
    both = jnp.concatenate([projected, onehot], axis=1)
    pair_send[...] = both.reshape(factor, tile_cols, tile_cols, 2 * bins)

    @pl.when(mirror_row == r)
    def _():
        pl.semaphore_wait(barrier, greeted - 1)

    @pl.when(mirror_row != r)
    def _():
        pl.semaphore_wait(barrier, greeted)

    def pair_each(k, act, own):
        alone = jnp.logical_and(mirror_row == r, r * factor + k == c)

        @pl.when(jnp.logical_not(alone))
        def _():
            act(k)

        if own is not None:
            @pl.when(alone)
            def _():
                own(k)

    def start_pair(k):
        pltpu.make_async_remote_copy(
            src_ref=pair_send.at[k],
            dst_ref=pair_recv.at[mirror_slab],
            send_sem=pair_ss.at[k],
            recv_sem=pair_rs.at[mirror_slab],
            device_id=(mirror_row, r * factor + k),
            device_id_type=MESH,
        ).start()

    def own_pair(k):
        pair_recv[k] = pair_send[k]

    def wait_pair(k):
        taken = pltpu.make_async_remote_copy(
            src_ref=pair_send.at[k],
            dst_ref=pair_recv.at[k],
            send_sem=pair_ss.at[k],
            recv_sem=pair_rs.at[k],
            device_id=(mirror_row, r * factor + k),
            device_id_type=MESH,
        )
        taken.wait_recv()
        taken.wait_send()

    for k in range(factor):
        pair_each(k, start_pair, own_pair)
    for k in range(factor):
        pair_each(k, wait_pair, None)

    mirrored = jnp.concatenate(
        [
            jnp.concatenate([pair_recv[k, :, i, :] for i in range(tile_cols)], axis=0)
            for k in range(factor)
        ],
        axis=0,
    )
    total = both + mirrored
    scores = total[:, :bins]
    highest = jnp.max(scores, axis=-1, keepdims=True)
    shifted = jnp.exp(scores - highest)
    exp_total = jnp.sum(shifted, axis=-1, keepdims=True)
    log_total = highest + jnp.log(exp_total)
    picked = jnp.sum(scores * onehot, axis=-1, keepdims=True)
    loss = jnp.sum(mask * (log_total - picked))
    count = jnp.sum(mask)
    d_sym = mask * (2.0 * (shifted / exp_total) - total[:, bins:])

    def core_copy(wave, src, dst):
        return remote(src, dst, core_ss, core_rs, wave, (r, sibling))

    def row_copies(wave, src, dst):
        return [
            remote(src((r + d) % R), dst.at[r], row_ss, row_rs, wave * (R - 1) + d - 1, ((r + d) % R, c))
            for d in range(1, R)
        ]

    def z_copies(wave, src, dst):
        return [
            remote(
                src((z + e) % Z), dst.at[z], z_ss, z_rs, wave * (Z - 1) + e - 1, (r, ((z + e) % Z) * 2 + core)
            )
            for e in range(1, Z)
        ]

    def start(copies):
        for copy in copies:
            copy.start()

    def finish(copies):
        for copy in copies:
            copy.wait()

    def add_up(ref, count):
        value = ref[0]
        for s in range(1, count):
            value = value + ref[s]
        return value

    def to_rows(wave, copy, own, got, across):
        copy.wait()
        got[...] = got[...] + own[:, :, core]
        copies = row_copies(wave, lambda s: got.at[s], across)
        start(copies)
        across[r] = got[r]
        return copies

    def to_z(wave, copies, across, kept, along):
        finish(copies)
        kept[...] = add_up(across, R)
        copies = z_copies(wave, lambda s: kept.at[s], along)
        start(copies)
        along[z] = kept[z]
        return copies

    pde_t = mm3(d_sym, updated, ((0,), (0,)))
    top = small.shape[2] - 8
    row_index = lax.broadcasted_iota(jnp.int32, (8, channels), 0)
    meta = jnp.where(row_index == 0, loss, jnp.where(row_index == 1, count, 0.0))
    for a in range(2):
        for b in range(R):
            q = a * R + b
            small[a, b, :nb, :] = pde_t[q * nb:(q + 1) * nb, :]
            small[a, b, top:, :] = meta
    small_c = core_copy(0, small.at[1 - core], small_core)
    small_c.start()

    d_updated = mm3(d_sym, w_pde, ((1,), (0,)))
    go[...] = mm3(hidden, d_updated, ((0,), (0,))).reshape(go.shape)
    go_c = core_copy(1, go.at[:, :, 1 - core], go_core)
    go_c.start()

    d_hidden = mm3(d_updated, wout_ref[...], ((1,), (1,)))
    small_c.wait()
    small_core[...] = small_core[...] + small[core]
    small_row[r] = small_core[r]
    small_r = row_copies(0, lambda s: small_core.at[s], small_row)
    start(small_r)

    d_up = d_hidden * silu
    d_gate = d_hidden * up * (sig * (1.0 + gate * (1.0 - sig)))
    d_proj = jnp.concatenate([d_gate, d_up], axis=1)
    go_r = to_rows(1, go_c, go, go_core, go_row)

    half = ga.shape[3]
    d_w_in = mm3(d_proj, normed, ((0,), (0,))).reshape(R, Z, 2, 2, half, channels)
    ga[...] = d_w_in[:, :, :, 0]
    gb[...] = d_w_in[:, :, :, 1]
    ga_c = core_copy(2, ga.at[:, :, 1 - core], ga_core)
    ga_c.start()
    gb_c = core_copy(4, gb.at[:, :, 1 - core], gb_core)
    gb_c.start()

    d_normed = mm3(d_proj, win_ref[...], ((1,), (0,)))
    d_gain = jnp.sum(d_normed * xhat, axis=0, keepdims=True)
    d_bias = jnp.sum(d_normed, axis=0, keepdims=True)
    norm[...] = jnp.where(row_index == 0, d_gain, jnp.where(row_index == 1, d_bias, 0.0))
    norm_c = core_copy(3, norm, norm_core)
    norm_c.start()

    ga_r = to_rows(2, ga_c, ga, ga_core, ga_row)
    gb_r = to_rows(4, gb_c, gb, gb_core, gb_row)

    norm_c.wait()
    norm_core[...] = norm_core[...] + norm[...]
    norm_row[r] = norm_core[...]
    norm_r = row_copies(3, lambda s: norm_core, norm_row)
    start(norm_r)

    d_xhat = d_normed * gain
    first = jnp.mean(d_xhat, axis=-1, keepdims=True)
    second = jnp.mean(d_xhat * xhat, axis=-1, keepdims=True)
    dx = rstd * (d_xhat - first - xhat * second) + d_updated

    finish(small_r)
    small_z[z] = add_up(small_row, R)
    small_zc = z_copies(0, lambda s: small_z.at[z], small_z)
    start(small_zc)
    go_zc = to_z(1, go_r, go_row, go_sum, go_z)
    finish(small_zc)
    reduced = add_up(small_z, Z)
    whole_count = reduced[top + 1:top + 2, :]
    inverse = 1.0 / whole_count
    mine = core * R + r
    small_last[mine] = reduced[:top]
    last = []
    for a in range(2):
        for d in range(R):
            if a or d:
                where = ((r + d) % R, z * 2 + (core + a) % 2)
                last.append(
                    remote(small_last.at[mine], small_last.at[mine], last_ss, last_rs, a * R + d - 1, where)
                )
    start(last)
    loss_out[...] = (reduced[top:top + 1, :] * inverse)[:, :1]
    dx_out[...] = dx * inverse

    ga_zc = to_z(2, ga_r, ga_row, ga_sum, ga_z)

    finish(norm_r)
    norm_z[z] = add_up(norm_row, R)
    norm_zc = z_copies(3, lambda s: norm_z.at[z], norm_z)
    start(norm_zc)

    gb_zc = to_z(4, gb_r, gb_row, gb_sum, gb_z)

    finish(go_zc)
    dout_out[...] = add_up(go_z, Z) * inverse
    finish(norm_zc)
    norm_all = add_up(norm_z, Z) * inverse
    gain_out[...] = norm_all[0:1]
    bias_out[...] = norm_all[1:2]
    finish(ga_zc)
    din_out[:half, :] = add_up(ga_z, Z) * inverse
    finish(gb_zc)
    din_out[half:, :] = add_up(gb_z, Z) * inverse
    finish(last)
    for q in range(2 * R):
        pde_out[q * nb:(q + 1) * nb, :] = small_last[q, :nb, :] * inverse


def put_out(*refs):
    sems = refs[-1]
    half = (len(refs) - 1) // 2
    copies = [
        pltpu.make_async_copy(refs[k], refs[half + k], sems.at[k]) for k in range(half)
    ]
    for copy in copies:
        copy.start()
    for copy in copies:
        copy.wait()


def on_device(pair_rep, ln_gain, ln_bias, w_in, w_out, w_pde, labels, pair_mask):
    tile_rows, tile_cols, channels = pair_rep.shape
    bins = w_pde.shape[1]
    R = lax.axis_size("row")
    Z = lax.axis_size("col") // 2
    owners = R * Z * 2
    pairs = tile_rows * tile_cols
    factor = tile_rows // tile_cols
    nb = bins // (2 * R)
    nbp = -(-nb // 8) * 8
    rows_i = w_in.shape[0] // owners
    rows_o = w_out.shape[0] // owners
    f32 = jnp.float32

    def vmem(*shape):
        return pltpu.VMEM(shape, f32)

    def wave(rows):
        return [
            vmem(R, Z, 2, rows, channels),
            vmem(R, Z, rows, channels),
            vmem(R, Z, rows, channels),
            vmem(Z, rows, channels),
            vmem(Z, rows, channels),
        ]

    dma = pltpu.SemaphoreType.DMA
    pair_send_shape = (factor, tile_cols, tile_cols, 2 * bins)
    scratch = [
        vmem(*pair_send_shape),
        vmem(*pair_send_shape),
        vmem(2, R, nbp + 8, channels),
        vmem(R, nbp + 8, channels),
        vmem(R, nbp + 8, channels),
        vmem(Z, nbp + 8, channels),
        vmem(2 * R, nbp, channels),
        vmem(8, channels),
        vmem(8, channels),
        vmem(R, 8, channels),
        vmem(Z, 8, channels),
        *wave(rows_o),
        *wave(rows_i // 2),
        *wave(rows_i // 2),
        vmem(pairs, channels),
        vmem(1, channels),
        vmem(1, channels),
        vmem(*w_in.shape),
        vmem(*w_out.shape),
        vmem(bins, channels),
        pltpu.VMEM((tile_cols, tile_rows), labels.dtype),
        pltpu.VMEM((tile_cols, tile_rows), pair_mask.dtype),
        dma((8,)),
        dma((factor,)),
        dma((factor,)),
        dma((5,)),
        dma((5,)),
        dma((5 * (R - 1),)),
        dma((5 * (R - 1),)),
        dma((5 * (Z - 1),)),
        dma((5 * (Z - 1),)),
        dma((2 * R - 1,)),
        dma((2 * R - 1,)),
    ]
    shape = jax.ShapeDtypeStruct
    held = pl.pallas_call(
        functools.partial(kernel, (R, Z, tile_rows, tile_cols, bins, nb)),
        out_shape=[
            vmem(1, 1),
            vmem(pairs, channels),
            vmem(1, channels),
            vmem(1, channels),
            vmem(rows_i, channels),
            vmem(rows_o, channels),
            vmem(bins, channels),
        ],
        in_specs=[pl.BlockSpec(memory_space=pl.ANY)] * 8,
        out_specs=[pl.BlockSpec(memory_space=pltpu.VMEM)] * 7,
        scratch_shapes=scratch,
        compiler_params=pltpu.CompilerParams(collective_id=0, has_side_effects=True),
        name="head_step",
    )(
        pair_rep.reshape(pairs, channels),
        ln_gain.reshape(1, channels),
        ln_bias.reshape(1, channels),
        w_in,
        w_out,
        w_pde.T,
        labels.T,
        pair_mask.T,
    )
    held = [pltpu.with_memory_space_constraint(value, pltpu.VMEM) for value in held]
    loss, dx, gain, bias, d_in, d_out, pde_t = pl.pallas_call(
        put_out,
        out_shape=[shape(value.shape, f32) for value in held],
        in_specs=[pl.BlockSpec(memory_space=pltpu.VMEM)] * 7,
        out_specs=[pl.BlockSpec(memory_space=pl.ANY)] * 7,
        scratch_shapes=[dma((7,))],
        name="put_out",
    )(*held)
    return (
        loss.reshape(()),
        dx.reshape(pair_rep.shape),
        gain.reshape(channels),
        bias.reshape(channels),
        d_in,
        d_out,
        pde_t.T,
    )


def solution(mesh):
    placed = (P("row", "col", None), P(), P(), P(), P(), P(), P("row", "col"), P("row", "col"))
    return jax.shard_map(
        on_device,
        mesh=mesh,
        in_specs=placed,
        out_specs=(
            P(),
            P("row", "col", None),
            P(),
            P(),
            P(("row", "col"), None),
            P(("row", "col"), None),
            P(),
        ),
        check_vma=False,
    )
```

```python
import functools

import jax
import jax.numpy as jnp
from jax import lax
from jax.experimental import pallas as pl
from jax.experimental.pallas import tpu as pltpu
from jax.sharding import PartitionSpec as P

epsilon = 1e-05
MESH = pl.DeviceIdType.MESH
HI = lax.Precision.HIGHEST


def mm(a, b, dims):
    return lax.dot_general(a, b, (dims, ((), ())), precision=HI, preferred_element_type=jnp.float32)


def dot_nn(a, b):
    return mm(a, b, ((1,), (0,)))


def dot_nt(a, b):
    return mm(a, b, ((1,), (1,)))


def dot_tn(a, b):
    return mm(a, b, ((0,), (0,)))


def two(value):
    high = value.astype(jnp.bfloat16)
    return high, (value - high.astype(jnp.float32)).astype(jnp.bfloat16)


def mm3(a, b, dims):
    a_high, a_low = two(a)
    b_high, b_low = two(b)

    def part(p, q):
        return lax.dot_general(p, q, (dims, ((), ())), preferred_element_type=jnp.float32)

    return part(a_high, b_high) + (part(a_high, b_low) + part(a_low, b_high))


def remote(src, dst, sends, recvs, slot, device):
    return pltpu.make_async_remote_copy(
        src_ref=src,
        dst_ref=dst,
        send_sem=sends.at[slot],
        recv_sem=recvs.at[slot],
        device_id=device,
        device_id_type=MESH,
    )


def spread(values, tile_rows, tile_cols):
    pairs = tile_rows * tile_cols
    values = values.T
    rows = jnp.broadcast_to(values[:, None, :], (tile_rows, tile_cols, tile_cols))
    rows = rows.reshape(pairs, tile_cols)
    place = lax.broadcasted_iota(jnp.int32, (pairs, tile_cols), 0) % tile_cols
    lane = lax.broadcasted_iota(jnp.int32, (pairs, tile_cols), 1)
    return jnp.sum(jnp.where(place == lane, rows, 0.0), axis=1, keepdims=True)


def kernel(
    sizes,
    x_hbm, gain_hbm, bias_hbm, win_hbm, wout_hbm, wpde_hbm, lab_hbm, mask_hbm,
    loss_out, dx_out, gain_out, bias_out, din_out, dout_out, pde_out,
    pair_send, pair_recv,
    small, small_core, small_row, small_z, small_last,
    norm, norm_core, norm_row, norm_z,
    go, go_core, go_row, go_sum, go_z,
    ga, ga_core, ga_row, ga_sum, ga_z,
    gb, gb_core, gb_row, gb_sum, gb_z,
    x_ref, gain_ref, bias_ref, win_ref, wout_ref, wpde_ref, lab_ref, mask_ref, load_sems,
    pair_ss, pair_rs, core_ss, core_rs, row_ss, row_rs, z_ss, z_rs, last_ss, last_rs,
):
    R, Z, tile_rows, tile_cols, bins, nb = sizes
    factor = tile_rows // tile_cols
    slab = tile_cols * tile_cols
    pairs = tile_rows * tile_cols
    r = lax.axis_index("row")
    c = lax.axis_index("col")
    core = c % 2
    z = c // 2
    sibling = z * 2 + 1 - core
    mirror_row = c // factor
    mirror_slab = c % factor
    channels = x_hbm.shape[1]
    hidden_units = wout_hbm.shape[0]

    barrier = pltpu.get_barrier_semaphore()

    def greet(row, col):
        pl.semaphore_signal(barrier, inc=1, device_id=(row, col), device_id_type=MESH)

    for k in range(factor):
        partner_col = r * factor + k

        @pl.when(jnp.logical_or(mirror_row != r, partner_col != c))
        def _():
            greet(mirror_row, partner_col)

    greet(r, sibling)
    for d in range(1, R):
        greet((r + d) % R, c)
        greet((r + d) % R, sibling)
    for e in range(1, Z):
        greet(r, ((z + e) % Z) * 2 + core)
    greeted = factor + 1 + 2 * (R - 1) + (Z - 1)

    loads = [
        pltpu.make_async_copy(source, target, load_sems.at[k])
        for k, (source, target) in enumerate(
            (
                (x_hbm, x_ref), (gain_hbm, gain_ref), (bias_hbm, bias_ref), (win_hbm, win_ref),
                (wout_hbm, wout_ref), (wpde_hbm, wpde_ref), (lab_hbm, lab_ref), (mask_hbm, mask_ref),
            )
        )
    ]
    for load in loads:
        load.start()

    for load in loads[:3]:
        load.wait()
    x = x_ref[...]
    gain = gain_ref[...]
    average = jnp.mean(x, axis=-1, keepdims=True)
    centred = x - average
    variance = jnp.mean(centred * centred, axis=-1, keepdims=True)
    rstd = lax.rsqrt(variance + epsilon)
    xhat = centred * rstd
    normed = xhat * gain + bias_ref[...]
    loads[3].wait()
    gate = dot_nt(normed, win_ref[:hidden_units, :])
    up = dot_nt(normed, win_ref[hidden_units:, :])
    sig = 1.0 / (1.0 + jnp.exp(-gate))
    silu = gate * sig
    hidden = silu * up
    loads[4].wait()
    updated = x + dot_nn(hidden, wout_ref[...])
    for load in loads[5:]:
        load.wait()
    w_pde = wpde_ref[...]
    projected = dot_nt(updated, w_pde)
    label = spread(lab_ref[...].astype(jnp.float32), tile_rows, tile_cols)
    mask = spread(mask_ref[...].astype(jnp.float32), tile_rows, tile_cols)
    bin_index = lax.broadcasted_iota(jnp.int32, (pairs, bins), 1).astype(jnp.float32)
    onehot = (bin_index == label).astype(jnp.float32)
    both = jnp.concatenate([projected, onehot], axis=1)
    pair_send[...] = both.reshape(factor, tile_cols, tile_cols, 2 * bins)

    @pl.when(mirror_row == r)
    def _():
        pl.semaphore_wait(barrier, greeted - 1)

    @pl.when(mirror_row != r)
    def _():
        pl.semaphore_wait(barrier, greeted)

    def pair_each(k, act, own):
        alone = jnp.logical_and(mirror_row == r, r * factor + k == c)

        @pl.when(jnp.logical_not(alone))
        def _():
            act(k)

        if own is not None:
            @pl.when(alone)
            def _():
                own(k)

    def start_pair(k):
        pltpu.make_async_remote_copy(
            src_ref=pair_send.at[k],
            dst_ref=pair_recv.at[mirror_slab],
            send_sem=pair_ss.at[k],
            recv_sem=pair_rs.at[mirror_slab],
            device_id=(mirror_row, r * factor + k),
            device_id_type=MESH,
        ).start()

    def own_pair(k):
        pair_recv[k] = pair_send[k]

    def wait_pair(k):
        taken = pltpu.make_async_remote_copy(
            src_ref=pair_send.at[k],
            dst_ref=pair_recv.at[k],
            send_sem=pair_ss.at[k],
            recv_sem=pair_rs.at[k],
            device_id=(mirror_row, r * factor + k),
            device_id_type=MESH,
        )
        taken.wait_recv()
        taken.wait_send()

    for k in range(factor):
        pair_each(k, start_pair, own_pair)
    for k in range(factor):
        pair_each(k, wait_pair, None)

    mirrored = jnp.concatenate(
        [
            jnp.concatenate([pair_recv[k, :, i, :] for i in range(tile_cols)], axis=0)
            for k in range(factor)
        ],
        axis=0,
    )
    total = both + mirrored
    scores = total[:, :bins]
    highest = jnp.max(scores, axis=-1, keepdims=True)
    shifted = jnp.exp(scores - highest)
    exp_total = jnp.sum(shifted, axis=-1, keepdims=True)
    log_total = highest + jnp.log(exp_total)
    picked = jnp.sum(scores * onehot, axis=-1, keepdims=True)
    loss = jnp.sum(mask * (log_total - picked))
    count = jnp.sum(mask)
    d_sym = mask * (2.0 * (shifted / exp_total) - total[:, bins:])

    def core_copy(wave, src, dst):
        return remote(src, dst, core_ss, core_rs, wave, (r, sibling))

    def row_copies(wave, src, dst):
        return [
            remote(src((r + d) % R), dst.at[r], row_ss, row_rs, wave * (R - 1) + d - 1, ((r + d) % R, c))
            for d in range(1, R)
        ]

    def z_copies(wave, src, dst):
        return [
            remote(
                src((z + e) % Z), dst.at[z], z_ss, z_rs, wave * (Z - 1) + e - 1, (r, ((z + e) % Z) * 2 + core)
            )
            for e in range(1, Z)
        ]

    def start(copies):
        for copy in copies:
            copy.start()

    def finish(copies):
        for copy in copies:
            copy.wait()

    def add_up(ref, count):
        value = ref[0]
        for s in range(1, count):
            value = value + ref[s]
        return value

    def to_rows(wave, copy, own, got, across):
        copy.wait()
        got[...] = got[...] + own[:, :, core]
        copies = row_copies(wave, lambda s: got.at[s], across)
        start(copies)
        across[r] = got[r]
        return copies

    def to_z(wave, copies, across, kept, along):
        finish(copies)
        kept[...] = add_up(across, R)
        copies = z_copies(wave, lambda s: kept.at[s], along)
        start(copies)
        along[z] = kept[z]
        return copies

    pde_t = mm3(d_sym, updated, ((0,), (0,)))
    top = small.shape[2] - 8
    row_index = lax.broadcasted_iota(jnp.int32, (8, channels), 0)
    meta = jnp.where(row_index == 0, loss, jnp.where(row_index == 1, count, 0.0))
    for a in range(2):
        for b in range(R):
            q = a * R + b
            small[a, b, :nb, :] = pde_t[q * nb:(q + 1) * nb, :]
            small[a, b, top:, :] = meta
    small_c = core_copy(0, small.at[1 - core], small_core)
    small_c.start()

    d_updated = mm3(d_sym, w_pde, ((1,), (0,)))
    go[...] = mm3(hidden, d_updated, ((0,), (0,))).reshape(go.shape)
    go_c = core_copy(1, go.at[:, :, 1 - core], go_core)
    go_c.start()

    d_hidden = mm3(d_updated, wout_ref[...], ((1,), (1,)))
    small_c.wait()
    small_core[...] = small_core[...] + small[core]
    small_row[r] = small_core[r]
    small_r = row_copies(0, lambda s: small_core.at[s], small_row)
    start(small_r)

    d_up = d_hidden * silu
    d_gate = d_hidden * up * (sig * (1.0 + gate * (1.0 - sig)))
    d_proj = jnp.concatenate([d_gate, d_up], axis=1)
    go_r = to_rows(1, go_c, go, go_core, go_row)

    half = ga.shape[3]
    d_w_in = mm3(d_proj, normed, ((0,), (0,))).reshape(R, Z, 2, 2, half, channels)
    ga[...] = d_w_in[:, :, :, 0]
    gb[...] = d_w_in[:, :, :, 1]
    ga_c = core_copy(2, ga.at[:, :, 1 - core], ga_core)
    ga_c.start()
    gb_c = core_copy(4, gb.at[:, :, 1 - core], gb_core)
    gb_c.start()

    d_normed = mm3(d_proj, win_ref[...], ((1,), (0,)))
    d_gain = jnp.sum(d_normed * xhat, axis=0, keepdims=True)
    d_bias = jnp.sum(d_normed, axis=0, keepdims=True)
    norm[...] = jnp.where(row_index == 0, d_gain, jnp.where(row_index == 1, d_bias, 0.0))
    norm_c = core_copy(3, norm, norm_core)
    norm_c.start()

    ga_r = to_rows(2, ga_c, ga, ga_core, ga_row)
    norm_c.wait()
    norm_core[...] = norm_core[...] + norm[...]
    norm_row[r] = norm_core[...]
    norm_r = row_copies(3, lambda s: norm_core, norm_row)
    start(norm_r)

    gb_r = to_rows(4, gb_c, gb, gb_core, gb_row)

    d_xhat = d_normed * gain
    first = jnp.mean(d_xhat, axis=-1, keepdims=True)
    second = jnp.mean(d_xhat * xhat, axis=-1, keepdims=True)
    dx = rstd * (d_xhat - first - xhat * second) + d_updated

    finish(small_r)
    small_z[z] = add_up(small_row, R)
    small_zc = z_copies(0, lambda s: small_z.at[z], small_z)
    start(small_zc)
    go_zc = to_z(1, go_r, go_row, go_sum, go_z)
    finish(small_zc)
    reduced = add_up(small_z, Z)
    whole_count = reduced[top + 1:top + 2, :]
    inverse = 1.0 / whole_count
    mine = core * R + r
    small_last[mine] = reduced[:top]
    last = []
    for a in range(2):
        for d in range(R):
            if a or d:
                where = ((r + d) % R, z * 2 + (core + a) % 2)
                last.append(
                    remote(small_last.at[mine], small_last.at[mine], last_ss, last_rs, a * R + d - 1, where)
                )
    start(last)
    loss_out[...] = (reduced[top:top + 1, :] * inverse)[:, :1]
    dx_out[...] = dx * inverse

    ga_zc = to_z(2, ga_r, ga_row, ga_sum, ga_z)

    finish(norm_r)
    norm_z[z] = add_up(norm_row, R)
    norm_zc = z_copies(3, lambda s: norm_z.at[z], norm_z)
    start(norm_zc)

    gb_zc = to_z(4, gb_r, gb_row, gb_sum, gb_z)

    finish(go_zc)
    dout_out[...] = add_up(go_z, Z) * inverse
    finish(norm_zc)
    norm_all = add_up(norm_z, Z) * inverse
    gain_out[...] = norm_all[0:1]
    bias_out[...] = norm_all[1:2]
    finish(ga_zc)
    din_out[:half, :] = add_up(ga_z, Z) * inverse
    finish(gb_zc)
    din_out[half:, :] = add_up(gb_z, Z) * inverse
    finish(last)
    for q in range(2 * R):
        pde_out[q * nb:(q + 1) * nb, :] = small_last[q, :nb, :] * inverse


def put_out(*refs):
    sems = refs[-1]
    half = (len(refs) - 1) // 2
    copies = [
        pltpu.make_async_copy(refs[k], refs[half + k], sems.at[k]) for k in range(half)
    ]
    for copy in copies:
        copy.start()
    for copy in copies:
        copy.wait()


def on_device(pair_rep, ln_gain, ln_bias, w_in, w_out, w_pde, labels, pair_mask):
    tile_rows, tile_cols, channels = pair_rep.shape
    bins = w_pde.shape[1]
    R = lax.axis_size("row")
    Z = lax.axis_size("col") // 2
    owners = R * Z * 2
    pairs = tile_rows * tile_cols
    factor = tile_rows // tile_cols
    nb = bins // (2 * R)
    nbp = -(-nb // 8) * 8
    rows_i = w_in.shape[0] // owners
    rows_o = w_out.shape[0] // owners
    f32 = jnp.float32

    def vmem(*shape):
        return pltpu.VMEM(shape, f32)

    def wave(rows):
        return [
            vmem(R, Z, 2, rows, channels),
            vmem(R, Z, rows, channels),
            vmem(R, Z, rows, channels),
            vmem(Z, rows, channels),
            vmem(Z, rows, channels),
        ]

    dma = pltpu.SemaphoreType.DMA
    pair_send_shape = (factor, tile_cols, tile_cols, 2 * bins)
    scratch = [
        vmem(*pair_send_shape),
        vmem(*pair_send_shape),
        vmem(2, R, nbp + 8, channels),
        vmem(R, nbp + 8, channels),
        vmem(R, nbp + 8, channels),
        vmem(Z, nbp + 8, channels),
        vmem(2 * R, nbp, channels),
        vmem(8, channels),
        vmem(8, channels),
        vmem(R, 8, channels),
        vmem(Z, 8, channels),
        *wave(rows_o),
        *wave(rows_i // 2),
        *wave(rows_i // 2),
        vmem(pairs, channels),
        vmem(1, channels),
        vmem(1, channels),
        vmem(*w_in.shape),
        vmem(*w_out.shape),
        vmem(bins, channels),
        pltpu.VMEM((tile_cols, tile_rows), labels.dtype),
        pltpu.VMEM((tile_cols, tile_rows), pair_mask.dtype),
        dma((8,)),
        dma((factor,)),
        dma((factor,)),
        dma((5,)),
        dma((5,)),
        dma((5 * (R - 1),)),
        dma((5 * (R - 1),)),
        dma((5 * (Z - 1),)),
        dma((5 * (Z - 1),)),
        dma((2 * R - 1,)),
        dma((2 * R - 1,)),
    ]
    shape = jax.ShapeDtypeStruct
    held = pl.pallas_call(
        functools.partial(kernel, (R, Z, tile_rows, tile_cols, bins, nb)),
        out_shape=[
            vmem(1, 1),
            vmem(pairs, channels),
            vmem(1, channels),
            vmem(1, channels),
            vmem(rows_i, channels),
            vmem(rows_o, channels),
            vmem(bins, channels),
        ],
        in_specs=[pl.BlockSpec(memory_space=pl.ANY)] * 8,
        out_specs=[pl.BlockSpec(memory_space=pltpu.VMEM)] * 7,
        scratch_shapes=scratch,
        compiler_params=pltpu.CompilerParams(collective_id=0, has_side_effects=True),
        name="head_step",
    )(
        pair_rep.reshape(pairs, channels),
        ln_gain.reshape(1, channels),
        ln_bias.reshape(1, channels),
        w_in,
        w_out,
        w_pde.T,
        labels.T,
        pair_mask.T,
    )
    held = [pltpu.with_memory_space_constraint(value, pltpu.VMEM) for value in held]
    loss, dx, gain, bias, d_in, d_out, pde_t = pl.pallas_call(
        put_out,
        out_shape=[shape(value.shape, f32) for value in held],
        in_specs=[pl.BlockSpec(memory_space=pltpu.VMEM)] * 7,
        out_specs=[pl.BlockSpec(memory_space=pl.ANY)] * 7,
        scratch_shapes=[dma((7,))],
        name="put_out",
    )(*held)
    return (
        loss.reshape(()),
        dx.reshape(pair_rep.shape),
        gain.reshape(channels),
        bias.reshape(channels),
        d_in,
        d_out,
        pde_t.T,
    )


def solution(mesh):
    placed = (P("row", "col", None), P(), P(), P(), P(), P(), P("row", "col"), P("row", "col"))
    return jax.shard_map(
        on_device,
        mesh=mesh,
        in_specs=placed,
        out_specs=(
            P(),
            P("row", "col", None),
            P(),
            P(),
            P(("row", "col"), None),
            P(("row", "col"), None),
            P(),
        ),
        check_vma=False,
    )
```
